256 devices in a mesh: occ: 16 (over x_lo, z), virt: 16 (over x_hi, y, core).
Axes of the slice: x: 4 (x_hi: 2, x_lo: 2; x = x_hi * 2 + x_lo), y: 4, z: 8, core: 2. Of those that a mesh axis runs over, the one named last changes fastest.
Arguments:
- factors: float32 [128, 512, 512], P('occ'), may hold values from -0.9 to 0.9
- occ_energy: float32 [128], replicated, may hold values from -3 to -0.5
- virt_energy: float32 [512], replicated, may hold values from 0.5 to 9.5
- pairing: int32 [2, 16], replicated, may hold values from 0 to 15, as said below
Outputs:
- pair_energy: float32 [2, 128], P(None, 'occ')
- gradient: float32 [128, 512, 512], P('occ', 'virt')
The draws below stay inside these ranges and needn't reach their ends.
Inputs may be any that keep to these rules, and one draw needn't show every extreme that they name: `pairing`: in every round each group's partner is another group whose partner is that group.
All inputs are finite; a program needn't handle non-finite values.
Results may differ from the reference program's by a relative error of at most 0.0001.
Values sent between devices are 32-bit elements; how exact they have to be, the bound alone decides.
No kernel may reach another device: no remote copies, remote signals or barrier semaphores. Data moves between devices by JAX's collectives and lax.ppermute only.
A program may use at most 128 MiB of HBM per device.

```python
import jax
import jax.numpy as jnp
from jax import lax

OG = 8
V = 512
NAUX = 512
ROUNDS = 2
GROUPS = 16
NOCC = 128


def draw_virt_energy(key, part):
    increments = jax.random.uniform(jax.random.fold_in(key, 7), (V,), jnp.float32, 0.5, 1.5) * (6.0 / V)
    return (0.5 + jnp.cumsum(increments)).astype(jnp.float32)


def draw_pairing(key, part):
    plan = []
    for round_index in range(ROUNDS):
        shuffled = jax.random.permutation(jax.random.fold_in(key, 11 + round_index), GROUPS).astype(jnp.int32)
        positions = jnp.arange(GROUPS, dtype=jnp.int32) ^ 1
        mates = shuffled[positions]
        partner_row = jnp.zeros((GROUPS,), jnp.int32).at[shuffled].set(mates)
        plan.append(partner_row)
    return jnp.stack(plan).astype(jnp.int32)


def block_scale(key, dims, split, low, largest):
    loudness, own = 1.0, jax.random.fold_in(key, 6)
    for dim, blocks in split:
        steps = jnp.exp(jax.random.uniform(jax.random.fold_in(own, dim), (blocks,), jnp.float32, low / len(split), largest / len(split)))
        loudness = loudness * jnp.repeat(steps, dims[dim] // blocks).reshape([-1 if axis == dim else 1 for axis in range(len(dims))])
    return loudness


def centred(own_key, dims, spread, most, cuts=(), held_as=jnp.bfloat16):
    result = jax.random.normal(own_key, dims, jnp.float32) * spread
    if len(cuts) > 0:
        result = block_scale(own_key, dims, cuts, -0.22, 0.18) * result
    return jnp.clip(result, min=-most, max=most).astype(held_as)


def setup_inputs(seed: int = 0) -> dict:
    streams_of = jax.random.split(jax.random.key(seed), 5)
    factors = centred(streams_of[0], (NOCC, V, NAUX), 0.15, 0.9, ((0, 16),), jnp.float32)
    occ_energy = jnp.clip(jax.random.uniform(streams_of[1], (NOCC,), jnp.float32, -3.0, -0.5), -3.0, -0.5)
    virt_energy = draw_virt_energy(jax.random.fold_in(streams_of[4], 71), 0)
    pairing = draw_pairing(jax.random.fold_in(streams_of[4], 71), 0)
    return dict(factors=factors, occ_energy=occ_energy, virt_energy=virt_energy, pairing=pairing)


def pair_block(own_part, mate_part, own_energy, mate_energy, virt_energy):
    highest = lax.Precision.HIGHEST
    coulomb = jnp.einsum('iap,jbp->iajb', own_part, mate_part, precision=highest)
    swapped = jnp.einsum('ibp,jap->iajb', own_part, mate_part, precision=highest)
    denominator = (virt_energy[None, :, None, None] + virt_energy[None, None, None, :]
                   - own_energy[:, None, None, None] - mate_energy[None, None, :, None])
    amplitude = -(2.0 * coulomb - swapped) / denominator
    energy = jnp.sum(amplitude * coulomb, axis=(1, 2, 3)) / (V * OG * V)
    grad_part = jnp.einsum('iajb,jbp->iap', amplitude, mate_part, precision=highest)
    return energy, grad_part


def reference(factors, occ_energy, virt_energy, pairing):
    grouped = factors.reshape(GROUPS, OG, V, NAUX)
    grouped_energy = occ_energy.reshape(GROUPS, OG)
    total_grad = jnp.zeros((GROUPS, OG, V, NAUX), jnp.float32)
    energy_rows = []
    for round_index in range(ROUNDS):
        def one_group(group_index):
            mate_index = pairing[round_index, group_index]
            return pair_block(grouped[group_index], grouped[mate_index],
                              grouped_energy[group_index], grouped_energy[mate_index], virt_energy)
        energy_now, grad_now = lax.map(one_group, jnp.arange(GROUPS, dtype=jnp.int32))
        total_grad = total_grad + grad_now
        energy_rows.append(energy_now.reshape(NOCC))
    return jnp.stack(energy_rows), total_grad.reshape(NOCC, V, NAUX)
```

```python
import jax
import jax.numpy as jnp
from jax import lax
from jax.experimental import pallas as pl
from jax.experimental.pallas import tpu as pltpu
from jax.sharding import PartitionSpec as P

OG = 8
V = 512
NAUX = 512
ROUNDS = 2
GROUPS = 16
COLS = 16
HALF = V // 2
PIECE = OG * V // COLS
PART = PIECE // GROUPS
SLAB = V // COLS
ROWS = SLAB * NAUX // 128
VMEM_LIMIT = 16 << 20


CORE, OTHERS = 1, (8, 2)


def swap(array, flip):
    return lax.ppermute(array, "virt", [(v, v ^ flip) for v in range(COLS)])


def split(x):
    high = x.astype(jnp.bfloat16)
    return high, (x - high.astype(jnp.float32)).astype(jnp.bfloat16)


def dot(x, y, y_dim):
    return lax.dot_general(x, y, (((1,), (y_dim,)), ((), ())), preferred_element_type=jnp.float32)


def at(half, parity):
    return pl.ds(pl.multiple_of((half + parity - 2 * half * parity) * HALF, HALF), HALF)


def call(kernel, out_shape, name, args, scratch=(), scalars=0, cost=None):
    vmem = pl.BlockSpec(memory_space=pltpu.VMEM)
    smem = pl.BlockSpec(memory_space=pltpu.SMEM)
    many = isinstance(out_shape, tuple)
    return pl.pallas_call(
        kernel,
        out_shape=out_shape,
        in_specs=[smem] * scalars + [vmem] * (len(args) - scalars),
        out_specs=(vmem,) * len(out_shape) if many else vmem,
        scratch_shapes=scratch,
        compiler_params=pltpu.CompilerParams(vmem_limit_bytes=VMEM_LIMIT),
        cost_estimate=cost,
        name=name,
    )(*args)


def shape(*dims, dtype=jnp.float32):
    return jax.ShapeDtypeStruct(dims, dtype)


def halves_kernel(place_ref, own_ref, out_ref):
    for k in range(2):
        for h in range(2):
            high, low = split(own_ref[k, at(h, place_ref[0]), :])
            out_ref[k, h * HALF : (h + 1) * HALF, :] = high
            out_ref[k, V + h * HALF : V + (h + 1) * HALF, :] = low


def pick_kernel(mates_ref, mixed_ref, out_ref):
    for g in range(GROUPS):
        for r in range(ROUNDS):
            out_ref[g, r * PART : (r + 1) * PART, :] = mixed_ref[mates_ref[r, g]]


def cut_kernel(both_ref, *out_refs):
    for g in range(GROUPS):
        for r in range(ROUNDS):
            out_refs[r][g * PART : (g + 1) * PART, :] = both_ref[g, r * PART : (r + 1) * PART, :]


def unit_kernel(number, last, place_ref, occ_ref, own_ref, near_ref, far_ref, *rest):
    column_ref, row_ref = rest[:2]
    before_ref = rest[2] if number > 0 else None
    energy_refs = rest[3:6] if last else ()
    scratch = rest[-6:]
    high, low = scratch[:2]
    coulombs, amplitudes = scratch[2:4], scratch[4:]
    grad_ref = rest[-7] if last else rest[-8]
    for h, ref in enumerate((near_ref, far_ref)):
        s = slice(h * HALF, (h + 1) * HALF)
        high[s, :], low[s, :] = split(ref[...])

    def coulomb(n):
        own = own_ref.at[n]
        for b in range(2):
            s = slice(b * HALF, (b + 1) * HALF)
            both = dot(own[...], high[s, :], 1)
            coulombs[n][:, s] = both[:V] + (both[V:] + dot(own[:V, :], low[s, :], 1))

    def amplitude(n):
        shift = occ_ref[place_ref[1 + n]] + occ_ref[place_ref[3 + number]]
        total = jnp.zeros((8, HALF), jnp.float32)
        for a in range(2):
            s = slice(a * HALF, (a + 1) * HALF)
            for b in range(2):
                t = slice(b * HALF, (b + 1) * HALF)
                here = coulombs[n][s, t]
                below = column_ref[s, :] + row_ref[:, t] - shift
                value = (coulombs[n][t, s].T - 2.0 * here) / below
                total = total + jnp.sum((value * here).reshape(HALF // 8, 8, HALF), axis=0)
                value_high, value_low = split(value)
                amplitudes[n][s, t] = value_high
                amplitudes[n][V + a * HALF : V + (a + 1) * HALF, t] = value_low
        return total[:, :128] + total[:, 128:]

    def gradient(n):
        for p in range(2):
            s = slice(p * HALF, (p + 1) * HALF)
            both = dot(amplitudes[n][...], high[:, s], 0)
            value = both[:V] + (both[V:] + dot(amplitudes[n][:V, :], low[:, s], 0))
            if before_ref is not None:
                value = value + before_ref[n, :, s]
            if not last:
                grad_ref[n, :, s] = value
                continue
            for t in range(COLS):
                to = t + place_ref[0] * (COLS // 2)
                to = to - jnp.where(to >= COLS, COLS, 0)
                for e in range(SLAB // 8):
                    for q in range(HALF // 128):
                        line = n * ROWS + (e * 4 + p * 2 + q) * 8
                        grad_ref[to, line : line + 8, :] = value[
                            t * SLAB + e * 8 : t * SLAB + e * 8 + 8, q * 128 : (q + 1) * 128
                        ]

    energies = []
    coulomb(0)
    coulomb(1)
    for n in range(2):
        energies.append(amplitude(n))
        gradient(n)
    if not last:
        for n in range(2):
            rest[-7][n] = energies[n]
        return
    line = lax.broadcasted_iota(jnp.int32, (8, 128), 0)
    table = jnp.zeros((8, 128), jnp.float32)
    for n in range(2):
        for r, value in (
            (0, energy_refs[0][n] + energy_refs[2][n]),
            (1, energy_refs[1][n] + energies[n]),
        ):
            table = jnp.where(line == 2 * r + n, jnp.sum(value, axis=0, keepdims=True), table)
    for t in range(COLS):
        grad_ref[t, 2 * ROWS :, :] = table


def unit(number, place, occ, own, near, far, column, row, before, energies=()):
    last = len(energies) > 0
    args = [place, occ, own, near, far, column, row]
    args += ([] if before is None else [before]) + list(energies)

    def body(*refs):
        unit_kernel(number, last, *refs)

    out = shape(COLS, 2 * ROWS + 8, 128)
    return call(
        body,
        out if last else (shape(2, V, NAUX), shape(2, 8, 128)),
        "unit",
        args,
        scratch=[pltpu.VMEM((V, NAUX), jnp.bfloat16)] * 2
        + [pltpu.VMEM((V, V), jnp.float32)] * 2
        + [pltpu.VMEM((2 * V, V), jnp.bfloat16)] * 2,
        scalars=2,
        cost=pl.CostEstimate(
            flops=24 * V * V * NAUX, bytes_accessed=16 * V * NAUX, transcendentals=0
        ),
    )


def finish_kernel(slabs_ref, grad_ref, energy_ref):
    line = lax.broadcasted_iota(jnp.int32, (8, 128), 0)
    lane = lax.broadcasted_iota(jnp.int32, (8, 128), 1)
    table = jnp.zeros((8, 128), jnp.float32)

    def added(sources, rows):
        values = [slabs_ref[s, rows, :] for s in sources]
        return (values[0] + values[1]) + (values[2] + values[3])

    for quad in range(2):
        for core in range(2):
            sources = [(quad ^ (y & 1)) * 8 + y * 2 + core for y in range(4)]
            energy = jnp.sum(added(sources, slice(2 * ROWS, 2 * ROWS + 8)), axis=1, keepdims=True)
            for n in range(2):
                i = quad * 4 + core * 2 + n
                for p in range(4):
                    for q in range(4):
                        at_row = n * ROWS + (4 * p + q) * 8
                        grad_ref[i, 8 * p : 8 * p + 8, q * 128 : (q + 1) * 128] = added(
                            sources, slice(at_row, at_row + 8)
                        )
                for r in range(ROUNDS):
                    value = energy[2 * r + n : 2 * r + n + 1]
                    table = jnp.where((line == r) & (lane == i), value, table)
    energy_ref[...] = table[:ROUNDS, :OG] * (1.0 / (V * OG * V))


def per_device(factors, occ_energy, virt_energy, pairing):
    group = lax.axis_index("occ")
    v = lax.axis_index("virt")
    core = v & 1
    y = (v >> 1) & 3
    x = v >> 3
    slab = lax.dynamic_slice_in_dim(factors.reshape(OG * V, NAUX), v * PIECE, PIECE, 0)
    mixed = lax.all_to_all(
        slab.reshape(GROUPS, PART, NAUX), "occ", split_axis=0, concat_axis=0, tiled=True
    )
    orbital = (x ^ (y & 1)) * 4 + core * 2
    mates = [pairing[r, group] * OG for r in range(ROUNDS)]
    j = x * 4 + y
    place = jnp.stack(
        [core, group * OG + orbital, group * OG + orbital + 1]
        + [mates[0] + j, mates[1] + j, mates[0] + (j ^ 4), mates[1] + (j ^ 1)]
    ).astype(jnp.int32)
    turned = lax.dynamic_slice_in_dim(
        jnp.concatenate([virt_energy, virt_energy]), core * HALF, V, 0
    )
    column, row = turned.reshape(V, 1), turned.reshape(1, V)
    own = call(
        halves_kernel,
        shape(2, 2 * V, NAUX, dtype=jnp.bfloat16),
        "halves",
        [place, lax.dynamic_slice_in_dim(factors, orbital, 2, 0)],
        scalars=1,
    )
    mixed, own, place, column, row = lax.optimization_barrier((mixed, own, place, column, row))
    picked = call(
        pick_kernel, shape(GROUPS, ROUNDS * PART, NAUX), "pick", [pairing, mixed], scalars=1
    )
    both = lax.all_to_all(picked, "occ", split_axis=0, concat_axis=0, tiled=True)
    pieces = call(cut_kernel, (shape(PIECE, NAUX),) * ROUNDS, "cut", [both])
    others = [swap(piece, flip) for piece, flip in zip(pieces, OTHERS)]
    grads, energies = None, []
    for r in range(ROUNDS):
        near, far = pieces[r], swap(pieces[r], CORE)
        grads, energy = unit(r, place, occ_energy, own, near, far, column, row, grads)
        energies.append(energy)
    *others, grads = lax.optimization_barrier((*others, grads))
    near, far = others[0], swap(others[0], CORE)
    grads, energy = unit(2, place, occ_energy, own, near, far, column, row, grads)
    energies.append(energy)
    near, far = others[1], swap(others[1], CORE)
    sent = unit(3, place, occ_energy, own, near, far, column, row, grads, energies)
    slabs = lax.all_to_all(sent, "virt", split_axis=0, concat_axis=0, tiled=True)
    gradient, pair_energy = call(
        finish_kernel, (shape(OG, SLAB, NAUX), shape(ROUNDS, OG)), "finish", [slabs]
    )
    return (pair_energy, gradient)


def solution(mesh):
    placed = (P("occ", None, None), P(), P(), P())
    return jax.shard_map(
        per_device,
        mesh=mesh,
        in_specs=placed,
        out_specs=(P(None, "occ"), P("occ", "virt", None)),
        check_vma=False,
    )
```

```python
import jax
import jax.numpy as jnp
from jax import lax
from jax.experimental import pallas as pl
from jax.experimental.pallas import tpu as pltpu
from jax.sharding import PartitionSpec as P

OG = 8
V = 512
NAUX = 512
ROUNDS = 2
GROUPS = 16
COLS = 16
HALF = V // 2
PIECE = OG * V // COLS
PART = PIECE // GROUPS
SLAB = V // COLS
ROWS = SLAB * NAUX // 128
VMEM_LIMIT = 24 << 20


CORE, OTHERS = 1, (8, 2)


def swap(array, flip):
    return lax.ppermute(array, "virt", [(v, v ^ flip) for v in range(COLS)])


def split(x):
    high = x.astype(jnp.bfloat16)
    return high, (x - high.astype(jnp.float32)).astype(jnp.bfloat16)


def dot(x, y, y_dim):
    return lax.dot_general(x, y, (((1,), (y_dim,)), ((), ())), preferred_element_type=jnp.float32)


def at(half, parity):
    return pl.ds(pl.multiple_of((half + parity - 2 * half * parity) * HALF, HALF), HALF)


def call(kernel, out_shape, name, args, scratch=(), scalars=0, cost=None):
    vmem = pl.BlockSpec(memory_space=pltpu.VMEM)
    smem = pl.BlockSpec(memory_space=pltpu.SMEM)
    many = isinstance(out_shape, tuple)
    return pl.pallas_call(
        kernel,
        out_shape=out_shape,
        in_specs=[smem] * scalars + [vmem] * (len(args) - scalars),
        out_specs=(vmem,) * len(out_shape) if many else vmem,
        scratch_shapes=scratch,
        compiler_params=pltpu.CompilerParams(vmem_limit_bytes=VMEM_LIMIT),
        cost_estimate=cost,
        name=name,
    )(*args)


def shape(*dims, dtype=jnp.float32):
    return jax.ShapeDtypeStruct(dims, dtype)


def halves_kernel(place_ref, own_ref, out_ref):
    for k in range(2):
        for h in range(2):
            high, low = split(own_ref[k, at(h, place_ref[0]), :])
            out_ref[k, h * HALF : (h + 1) * HALF, :] = high
            out_ref[k, V + h * HALF : V + (h + 1) * HALF, :] = low


def pick_kernel(mates_ref, mixed_ref, out_ref):
    for g in range(GROUPS):
        for r in range(ROUNDS):
            out_ref[g, r * PART : (r + 1) * PART, :] = mixed_ref[mates_ref[r, g]]


def cut_kernel(both_ref, *out_refs):
    for g in range(GROUPS):
        for r in range(ROUNDS):
            out_refs[r][g * PART : (g + 1) * PART, :] = both_ref[g, r * PART : (r + 1) * PART, :]


def product(own, high, low):
    both = dot(own[...], high, 1)
    return both[:V] + (both[V:] + dot(own[:V, :], low, 1))


def near_kernel(own_ref, *refs):
    mates, out_ref = refs[:ROUNDS], refs[ROUNDS]
    for r in range(ROUNDS):
        high, low = split(mates[r][...])
        for n in range(2):
            out_ref[2 * r + n] = product(own_ref.at[n], high, low)


def unit_kernel(stage, place_ref, occ_ref, own_ref, *rest):
    mates, rest = rest[: 2 * ROUNDS], rest[2 * ROUNDS :]
    column_ref, row_ref = rest[:2]
    last = stage > 0
    if last:
        started_ref, before_ref, early_ref, grad_ref = rest[2:6]
    else:
        grad_ref, energy_ref = rest[2:4]
    high, low, coulombs, amplitudes = rest[-4:]
    for m, ref in enumerate(mates):
        s = slice(m * HALF, (m + 1) * HALF)
        high[s, :], low[s, :] = split(ref[...])

    def coulomb(n):
        for r in range(ROUNDS):
            for b in range(1 if last else 0, 2):
                s = slice((2 * r + b) * HALF, (2 * r + b + 1) * HALF)
                coulombs[n, :, s] = product(own_ref.at[n], high[s, :], low[s, :])

    def block(n, r, a, b):
        s = slice(a * HALF, (a + 1) * HALF)
        if last and b == 0:
            return started_ref[2 * r + n, s, :]
        return coulombs[n, s, (2 * r + b) * HALF : (2 * r + b + 1) * HALF]

    def amplitude(n):
        totals = []
        for r in range(ROUNDS):
            shift = occ_ref[place_ref[1 + n]] + occ_ref[place_ref[3 + 2 * stage + r]]
            total = jnp.zeros((8, HALF), jnp.float32)
            for a in range(2):
                s = slice(a * HALF, (a + 1) * HALF)
                for b in range(2):
                    here = block(n, r, a, b)
                    below = column_ref[s, :] + row_ref[:, b * HALF : (b + 1) * HALF] - shift
                    value = (block(n, r, b, a).T - 2.0 * here) / below
                    total = total + jnp.sum((value * here).reshape(HALF // 8, 8, HALF), axis=0)
                    value_high, value_low = split(value)
                    t = slice((2 * r + b) * HALF, (2 * r + b + 1) * HALF)
                    amplitudes[n, s, t] = value_high
                    amplitudes[n, V + a * HALF : V + (a + 1) * HALF, t] = value_low
            totals.append(total[:, :128] + total[:, 128:])
        return totals

    def gradient(n):
        for p in range(2):
            s = slice(p * HALF, (p + 1) * HALF)
            both = dot(amplitudes[n], high[:, s], 0)
            value = both[:V] + (both[V:] + dot(amplitudes[n, :V, :], low[:, s], 0))
            if not last:
                grad_ref[n, :, s] = value
                continue
            value = value + before_ref[n, :, s]
            for t in range(COLS):
                to = t + place_ref[0] * (COLS // 2)
                to = to - jnp.where(to >= COLS, COLS, 0)
                for e in range(SLAB // 8):
                    for q in range(HALF // 128):
                        line = n * ROWS + (e * 4 + p * 2 + q) * 8
                        grad_ref[to, line : line + 8, :] = value[
                            t * SLAB + e * 8 : t * SLAB + e * 8 + 8, q * 128 : (q + 1) * 128
                        ]

    energies = []
    coulomb(0)
    coulomb(1)
    for n in range(2):
        energies.append(amplitude(n))
        gradient(n)
    if not last:
        for n in range(2):
            for r in range(ROUNDS):
                energy_ref[2 * r + n] = energies[n][r]
        return
    line = lax.broadcasted_iota(jnp.int32, (8, 128), 0)
    table = jnp.zeros((8, 128), jnp.float32)
    for n in range(2):
        for r in range(ROUNDS):
            value = jnp.sum(early_ref[2 * r + n] + energies[n][r], axis=0, keepdims=True)
            table = jnp.where(line == 2 * r + n, value, table)
    for t in range(COLS):
        grad_ref[t, 2 * ROWS :, :] = table


def unit(stage, *args):
    def body(*refs):
        unit_kernel(stage, *refs)

    early = (shape(2, V, NAUX), shape(2 * ROUNDS, 8, 128))
    return call(
        body,
        shape(COLS, 2 * ROWS + 8, 128) if stage else early,
        "unit",
        args,
        scratch=[pltpu.VMEM((ROUNDS * V, NAUX), jnp.bfloat16)] * 2
        + [pltpu.VMEM((2, V, ROUNDS * V), jnp.float32)]
        + [pltpu.VMEM((2, 2 * V, ROUNDS * V), jnp.bfloat16)],
        scalars=2,
        cost=pl.CostEstimate(
            flops=48 * V * V * NAUX, bytes_accessed=16 * V * NAUX, transcendentals=0
        ),
    )


def finish_kernel(slabs_ref, grad_ref, energy_ref):
    line = lax.broadcasted_iota(jnp.int32, (8, 128), 0)
    lane = lax.broadcasted_iota(jnp.int32, (8, 128), 1)
    table = jnp.zeros((8, 128), jnp.float32)

    def added(sources, rows):
        values = [slabs_ref[s, rows, :] for s in sources]
        return (values[0] + values[1]) + (values[2] + values[3])

    for quad in range(2):
        for core in range(2):
            sources = [(quad ^ (y & 1)) * 8 + y * 2 + core for y in range(4)]
            energy = jnp.sum(added(sources, slice(2 * ROWS, 2 * ROWS + 8)), axis=1, keepdims=True)
            for n in range(2):
                i = quad * 4 + core * 2 + n
                for p in range(4):
                    for q in range(4):
                        at_row = n * ROWS + (4 * p + q) * 8
                        grad_ref[i, 8 * p : 8 * p + 8, q * 128 : (q + 1) * 128] = added(
                            sources, slice(at_row, at_row + 8)
                        )
                for r in range(ROUNDS):
                    value = energy[2 * r + n : 2 * r + n + 1]
                    table = jnp.where((line == r) & (lane == i), value, table)
    energy_ref[...] = table[:ROUNDS, :OG] * (1.0 / (V * OG * V))


def per_device(factors, occ_energy, virt_energy, pairing):
    group = lax.axis_index("occ")
    v = lax.axis_index("virt")
    core = v & 1
    y = (v >> 1) & 3
    x = v >> 3
    slab = lax.dynamic_slice_in_dim(factors.reshape(OG * V, NAUX), v * PIECE, PIECE, 0)
    mixed = lax.all_to_all(
        slab.reshape(GROUPS, PART, NAUX), "occ", split_axis=0, concat_axis=0, tiled=True
    )
    orbital = (x ^ (y & 1)) * 4 + core * 2
    mates = [pairing[r, group] * OG for r in range(ROUNDS)]
    j = x * 4 + y
    place = jnp.stack(
        [core, group * OG + orbital, group * OG + orbital + 1]
        + [mates[0] + j, mates[1] + j, mates[0] + (j ^ 4), mates[1] + (j ^ 1)]
    ).astype(jnp.int32)
    turned = lax.dynamic_slice_in_dim(
        jnp.concatenate([virt_energy, virt_energy]), core * HALF, V, 0
    )
    column, row = turned.reshape(V, 1), turned.reshape(1, V)
    own = call(
        halves_kernel,
        shape(2, 2 * V, NAUX, dtype=jnp.bfloat16),
        "halves",
        [place, lax.dynamic_slice_in_dim(factors, orbital, 2, 0)],
        scalars=1,
    )
    mixed, own, place, column, row = lax.optimization_barrier((mixed, own, place, column, row))
    picked = call(
        pick_kernel, shape(GROUPS, ROUNDS * PART, NAUX), "pick", [pairing, mixed], scalars=1
    )
    both = lax.all_to_all(picked, "occ", split_axis=0, concat_axis=0, tiled=True)
    pieces = call(cut_kernel, (shape(PIECE, NAUX),) * ROUNDS, "cut", [both])
    others = [swap(piece, flip) for piece, flip in zip(pieces, OTHERS)]
    mates = []
    for piece in pieces:
        mates += [piece, swap(piece, CORE)]
    grads, energy = unit(0, place, occ_energy, own, *mates, column, row)
    *others, grads = lax.optimization_barrier((*others, grads))
    mates = []
    for piece in others:
        mates += [piece, swap(piece, CORE)]
    started = call(
        near_kernel,
        shape(2 * ROUNDS, V, HALF),
        "near",
        [own, *others],
        cost=pl.CostEstimate(
            flops=12 * V * V * NAUX, bytes_accessed=4 * V * NAUX, transcendentals=0
        ),
    )
    sent = unit(1, place, occ_energy, own, *mates, column, row, started, grads, energy)
    slabs = lax.all_to_all(sent, "virt", split_axis=0, concat_axis=0, tiled=True)
    gradient, pair_energy = call(
        finish_kernel, (shape(OG, SLAB, NAUX), shape(ROUNDS, OG)), "finish", [slabs]
    )
    return (pair_energy, gradient)


def solution(mesh):
    placed = (P("occ", None, None), P(), P(), P())
    return jax.shard_map(
        per_device,
        mesh=mesh,
        in_specs=placed,
        out_specs=(P(None, "occ"), P("occ", "virt", None)),
        check_vma=False,
    )
```

```python
import jax
import jax.numpy as jnp
from jax import lax
from jax.experimental import pallas as pl
from jax.experimental.pallas import tpu as pltpu
from jax.sharding import PartitionSpec as P

OG = 8
V = 512
NAUX = 512
ROUNDS = 2
GROUPS = 16
COLS = 16
HALF = V // 2
PIECE = OG * V // COLS
PART = PIECE // GROUPS
SLAB = V // COLS
ROWS = SLAB * NAUX // 128
VMEM_LIMIT = 24 << 20


CORE, OTHERS = 1, (2, 6)


def swap(array, flip):
    return lax.ppermute(array, "virt", [(v, v ^ flip) for v in range(COLS)])


def split(x):
    high = x.astype(jnp.bfloat16)
    return high, (x - high.astype(jnp.float32)).astype(jnp.bfloat16)


def dot(x, y, y_dim):
    return lax.dot_general(x, y, (((1,), (y_dim,)), ((), ())), preferred_element_type=jnp.float32)


def at(half, parity):
    return pl.ds(pl.multiple_of((half + parity - 2 * half * parity) * HALF, HALF), HALF)


def call(kernel, out_shape, name, args, scratch=(), scalars=0, cost=None):
    vmem = pl.BlockSpec(memory_space=pltpu.VMEM)
    smem = pl.BlockSpec(memory_space=pltpu.SMEM)
    many = isinstance(out_shape, tuple)
    return pl.pallas_call(
        kernel,
        out_shape=out_shape,
        in_specs=[smem] * scalars + [vmem] * (len(args) - scalars),
        out_specs=(vmem,) * len(out_shape) if many else vmem,
        scratch_shapes=scratch,
        compiler_params=pltpu.CompilerParams(vmem_limit_bytes=VMEM_LIMIT),
        cost_estimate=cost,
        name=name,
    )(*args)


def shape(*dims, dtype=jnp.float32):
    return jax.ShapeDtypeStruct(dims, dtype)


def halves_kernel(place_ref, own_ref, out_ref):
    for k in range(2):
        for h in range(2):
            high, low = split(own_ref[k, at(h, place_ref[0]), :])
            out_ref[k, h * HALF : (h + 1) * HALF, :] = high
            out_ref[k, V + h * HALF : V + (h + 1) * HALF, :] = low


def pick_kernel(mates_ref, mixed_ref, out_ref):
    for g in range(GROUPS):
        for r in range(ROUNDS):
            out_ref[g, r * PART : (r + 1) * PART, :] = mixed_ref[mates_ref[r, g]]


def cut_kernel(both_ref, *out_refs):
    for g in range(GROUPS):
        for r in range(ROUNDS):
            out_refs[r][g * PART : (g + 1) * PART, :] = both_ref[g, r * PART : (r + 1) * PART, :]


def product(own, high, low):
    both = dot(own[...], high, 1)
    return both[:V] + (both[V:] + dot(own[:V, :], low, 1))


def near_kernel(own_ref, *refs):
    mates, out_ref = refs[:ROUNDS], refs[ROUNDS]
    for r in range(ROUNDS):
        high, low = split(mates[r][...])
        for n in range(2):
            out_ref[2 * r + n] = product(own_ref.at[n], high, low)


def unit_kernel(stage, place_ref, occ_ref, own_ref, *rest):
    mates, rest = rest[: 2 * ROUNDS], rest[2 * ROUNDS :]
    column_ref, row_ref = rest[:2]
    last = stage > 0
    if last:
        started_ref, before_ref, early_ref, grad_ref = rest[2:6]
    else:
        grad_ref, energy_ref = rest[2:4]
    high, low, coulombs, amplitudes = rest[-4:]
    for m, ref in enumerate(mates):
        s = slice(m * HALF, (m + 1) * HALF)
        high[s, :], low[s, :] = split(ref[...])

    def coulomb(n):
        for r in range(ROUNDS):
            for b in range(1 if last else 0, 2):
                s = slice((2 * r + b) * HALF, (2 * r + b + 1) * HALF)
                coulombs[n, :, s] = product(own_ref.at[n], high[s, :], low[s, :])

    def block(n, r, a, b):
        s = slice(a * HALF, (a + 1) * HALF)
        if last and b == 0:
            return started_ref[2 * r + n, s, :]
        return coulombs[n, s, (2 * r + b) * HALF : (2 * r + b + 1) * HALF]

    def amplitude(n):
        totals = []
        for r in range(ROUNDS):
            shift = occ_ref[place_ref[1 + n]] + occ_ref[place_ref[3 + 2 * stage + r]]
            total = jnp.zeros((8, HALF), jnp.float32)
            for a in range(2):
                s = slice(a * HALF, (a + 1) * HALF)
                for b in range(2):
                    here = block(n, r, a, b)
                    below = column_ref[s, :] + row_ref[:, b * HALF : (b + 1) * HALF] - shift
                    value = (block(n, r, b, a).T - 2.0 * here) / below
                    total = total + jnp.sum((value * here).reshape(HALF // 8, 8, HALF), axis=0)
                    value_high, value_low = split(value)
                    t = slice((2 * r + b) * HALF, (2 * r + b + 1) * HALF)
                    amplitudes[n, s, t] = value_high
                    amplitudes[n, V + a * HALF : V + (a + 1) * HALF, t] = value_low
            totals.append(total[:, :128] + total[:, 128:])
        return totals

    def gradient(n):
        for p in range(2):
            s = slice(p * HALF, (p + 1) * HALF)
            both = dot(amplitudes[n], high[:, s], 0)
            value = both[:V] + (both[V:] + dot(amplitudes[n, :V, :], low[:, s], 0))
            if not last:
                grad_ref[n, :, s] = value
                continue
            value = value + before_ref[n, :, s]
            for t in range(COLS):
                to = t + place_ref[0] * (COLS // 2)
                to = to - jnp.where(to >= COLS, COLS, 0)
                for e in range(SLAB // 8):
                    for q in range(HALF // 128):
                        line = n * ROWS + (e * 4 + p * 2 + q) * 8
                        grad_ref[to, line : line + 8, :] = value[
                            t * SLAB + e * 8 : t * SLAB + e * 8 + 8, q * 128 : (q + 1) * 128
                        ]

    energies = []
    coulomb(0)
    coulomb(1)
    for n in range(2):
        energies.append(amplitude(n))
        gradient(n)
    if not last:
        for n in range(2):
            for r in range(ROUNDS):
                energy_ref[2 * r + n] = energies[n][r]
        return
    line = lax.broadcasted_iota(jnp.int32, (8, 128), 0)
    table = jnp.zeros((8, 128), jnp.float32)
    for n in range(2):
        for r in range(ROUNDS):
            value = jnp.sum(early_ref[2 * r + n] + energies[n][r], axis=0, keepdims=True)
            table = jnp.where(line == 2 * r + n, value, table)
    for t in range(COLS):
        grad_ref[t, 2 * ROWS :, :] = table


def unit(stage, *args):
    def body(*refs):
        unit_kernel(stage, *refs)

    early = (shape(2, V, NAUX), shape(2 * ROUNDS, 8, 128))
    return call(
        body,
        shape(COLS, 2 * ROWS + 8, 128) if stage else early,
        "unit",
        args,
        scratch=[pltpu.VMEM((ROUNDS * V, NAUX), jnp.bfloat16)] * 2
        + [pltpu.VMEM((2, V, ROUNDS * V), jnp.float32)]
        + [pltpu.VMEM((2, 2 * V, ROUNDS * V), jnp.bfloat16)],
        scalars=2,
        cost=pl.CostEstimate(
            flops=48 * V * V * NAUX, bytes_accessed=16 * V * NAUX, transcendentals=0
        ),
    )


def finish_kernel(slabs_ref, grad_ref, energy_ref):
    step = pl.program_id(0)
    quad, core = step // 2, step % 2
    line = lax.broadcasted_iota(jnp.int32, (8, 128), 0)
    lane = lax.broadcasted_iota(jnp.int32, (8, 128), 1)
    table = jnp.zeros((8, 128), jnp.float32)
    sources = [x * 8 + y * 4 + quad * 2 + core for x in range(2) for y in range(2)]

    def added(rows):
        values = [slabs_ref[s, rows, :] for s in sources]
        return (values[0] + values[1]) + (values[2] + values[3])

    energy = jnp.sum(added(slice(2 * ROWS, 2 * ROWS + 8)), axis=1, keepdims=True)
    for n in range(2):
        for p in range(4):
            for q in range(4):
                at_row = n * ROWS + (4 * p + q) * 8
                grad_ref[n, 8 * p : 8 * p + 8, q * 128 : (q + 1) * 128] = added(
                    slice(at_row, at_row + 8)
                )
        for r in range(ROUNDS):
            value = energy[2 * r + n : 2 * r + n + 1]
            table = jnp.where((line == r) & (lane == 2 * step + n), value, table)
    table = table[:ROUNDS, :OG] * (1.0 / (V * OG * V))

    @pl.when(step == 0)
    def _():
        energy_ref[...] = table

    @pl.when(step > 0)
    def _():
        energy_ref[...] = energy_ref[...] + table


def finish(slabs):
    return pl.pallas_call(
        finish_kernel,
        out_shape=(shape(OG, SLAB, NAUX), shape(ROUNDS, OG)),
        grid=(OG // 2,),
        in_specs=[pl.BlockSpec(memory_space=pltpu.VMEM)],
        out_specs=(
            pl.BlockSpec((2, SLAB, NAUX), lambda p: (p, 0, 0)),
            pl.BlockSpec((ROUNDS, OG), lambda p: (0, 0)),
        ),
        compiler_params=pltpu.CompilerParams(vmem_limit_bytes=VMEM_LIMIT),
        name="finish",
    )(slabs)


def per_device(factors, occ_energy, virt_energy, pairing):
    group = lax.axis_index("occ")
    v = lax.axis_index("virt")
    core = v & 1
    y = (v >> 1) & 3
    x = v >> 3
    slab = lax.dynamic_slice_in_dim(factors.reshape(OG * V, NAUX), v * PIECE, PIECE, 0)
    mixed = lax.all_to_all(
        slab.reshape(GROUPS, PART, NAUX), "occ", split_axis=0, concat_axis=0, tiled=True
    )
    orbital = (y & 1) * 4 + core * 2
    mates = [pairing[r, group] * OG for r in range(ROUNDS)]
    j = x * 4 + y
    place = jnp.stack(
        [core, group * OG + orbital, group * OG + orbital + 1]
        + [mates[0] + j, mates[1] + j, mates[0] + (j ^ 1), mates[1] + (j ^ 3)]
    ).astype(jnp.int32)
    turned = lax.dynamic_slice_in_dim(
        jnp.concatenate([virt_energy, virt_energy]), core * HALF, V, 0
    )
    column, row = turned.reshape(V, 1), turned.reshape(1, V)
    own = call(
        halves_kernel,
        shape(2, 2 * V, NAUX, dtype=jnp.bfloat16),
        "halves",
        [place, lax.dynamic_slice_in_dim(factors, orbital, 2, 0)],
        scalars=1,
    )
    mixed, own, place, column, row = lax.optimization_barrier((mixed, own, place, column, row))
    picked = call(
        pick_kernel, shape(GROUPS, ROUNDS * PART, NAUX), "pick", [pairing, mixed], scalars=1
    )
    both = lax.all_to_all(picked, "occ", split_axis=0, concat_axis=0, tiled=True)
    pieces = call(cut_kernel, (shape(PIECE, NAUX),) * ROUNDS, "cut", [both])
    others = [swap(piece, flip) for piece, flip in zip(pieces, OTHERS)]
    mates = []
    for piece in pieces:
        mates += [piece, swap(piece, CORE)]
    grads, energy = unit(0, place, occ_energy, own, *mates, column, row)
    *others, grads = lax.optimization_barrier((*others, grads))
    mates = []
    for piece in others:
        mates += [piece, swap(piece, CORE)]
    started = call(
        near_kernel,
        shape(2 * ROUNDS, V, HALF),
        "near",
        [own, *others],
        cost=pl.CostEstimate(
            flops=12 * V * V * NAUX, bytes_accessed=4 * V * NAUX, transcendentals=0
        ),
    )
    sent = unit(1, place, occ_energy, own, *mates, column, row, started, grads, energy)
    slabs = lax.all_to_all(sent, "virt", split_axis=0, concat_axis=0, tiled=True)
    gradient, pair_energy = finish(slabs)
    return (pair_energy, gradient)


def solution(mesh):
    placed = (P("occ", None, None), P(), P(), P())
    return jax.shard_map(
        per_device,
        mesh=mesh,
        in_specs=placed,
        out_specs=(P(None, "occ"), P("occ", "virt", None)),
        check_vma=False,
    )
```

```python
import jax
import jax.numpy as jnp
from jax import lax
from jax.experimental import pallas as pl
from jax.experimental.pallas import tpu as pltpu
from jax.sharding import PartitionSpec as P

OG = 8
V = 512
NAUX = 512
ROUNDS = 2
GROUPS = 16
COLS = 16
HALF = V // 2
PIECE = OG * V // COLS
PART = PIECE // GROUPS
SLAB = V // COLS
ROWS = SLAB * NAUX // 128
VMEM_LIMIT = 24 << 20


CORE, OTHERS = 1, (2, 6)


def swap(array, flip):
    return lax.ppermute(array, "virt", [(v, v ^ flip) for v in range(COLS)])


def split(x):
    high = x.astype(jnp.bfloat16)
    return high, (x - high.astype(jnp.float32)).astype(jnp.bfloat16)


def dot(x, y, y_dim):
    return lax.dot_general(x, y, (((1,), (y_dim,)), ((), ())), preferred_element_type=jnp.float32)


def at(half, parity):
    return pl.ds(pl.multiple_of((half + parity - 2 * half * parity) * HALF, HALF), HALF)


def call(kernel, out_shape, name, args, scratch=(), scalars=0, cost=None):
    vmem = pl.BlockSpec(memory_space=pltpu.VMEM)
    smem = pl.BlockSpec(memory_space=pltpu.SMEM)
    many = isinstance(out_shape, tuple)
    return pl.pallas_call(
        kernel,
        out_shape=out_shape,
        in_specs=[smem] * scalars + [vmem] * (len(args) - scalars),
        out_specs=(vmem,) * len(out_shape) if many else vmem,
        scratch_shapes=scratch,
        compiler_params=pltpu.CompilerParams(vmem_limit_bytes=VMEM_LIMIT),
        cost_estimate=cost,
        name=name,
    )(*args)


def shape(*dims, dtype=jnp.float32):
    return jax.ShapeDtypeStruct(dims, dtype)


def halves_kernel(place_ref, own_ref, out_ref):
    for k in range(2):
        for h in range(2):
            high, low = split(own_ref[k, at(h, place_ref[0]), :])
            out_ref[k, h * HALF : (h + 1) * HALF, :] = high
            out_ref[k, V + h * HALF : V + (h + 1) * HALF, :] = low


def pick_kernel(mates_ref, mixed_ref, out_ref):
    for g in range(GROUPS):
        for r in range(ROUNDS):
            out_ref[g, r * PART : (r + 1) * PART, :] = mixed_ref[mates_ref[r, g]]


def cut_kernel(both_ref, *out_refs):
    for g in range(GROUPS):
        for r in range(ROUNDS):
            rows = both_ref[g, r * PART : (r + 1) * PART, :]
            out_refs[r][g * PART : (g + 1) * PART, :] = rows
            out_refs[ROUNDS][r, g * PART : (g + 1) * PART, :] = rows


def product(own, high, low):
    both = dot(own[...], high, 1)
    return both[:V] + (both[V:] + dot(own[:V, :], low, 1))


def near_kernel(own_ref, *refs):
    mates, out_ref = refs[:ROUNDS], refs[ROUNDS]
    for r in range(ROUNDS):
        high, low = split(mates[r][...])
        for n in range(2):
            out_ref[2 * r + n] = product(own_ref.at[n], high, low)


def unit_kernel(stage, place_ref, occ_ref, own_ref, *rest):
    mates, rest = rest[: 2 * ROUNDS], rest[2 * ROUNDS :]
    column_ref, row_ref = rest[:2]
    last = stage > 0
    if last:
        started_ref, before_ref, early_ref, grad_ref = rest[2:6]
    else:
        grad_ref, energy_ref = rest[2:4]
    high, low, coulombs, amplitudes = rest[-4:]
    for m, ref in enumerate(mates):
        s = slice(m * HALF, (m + 1) * HALF)
        high[s, :], low[s, :] = split(ref[...] if len(ref.shape) == 2 else ref[m // 2])

    def coulomb(n):
        for r in range(ROUNDS):
            for b in range(1 if last else 0, 2):
                s = slice((2 * r + b) * HALF, (2 * r + b + 1) * HALF)
                coulombs[n, :, s] = product(own_ref.at[n], high[s, :], low[s, :])

    def block(n, r, a, b):
        s = slice(a * HALF, (a + 1) * HALF)
        if last and b == 0:
            return started_ref[2 * r + n, s, :]
        return coulombs[n, s, (2 * r + b) * HALF : (2 * r + b + 1) * HALF]

    def amplitude(n):
        totals = []
        for r in range(ROUNDS):
            shift = occ_ref[place_ref[1 + n]] + occ_ref[place_ref[3 + 2 * stage + r]]
            total = jnp.zeros((8, HALF), jnp.float32)
            for a in range(2):
                s = slice(a * HALF, (a + 1) * HALF)
                for b in range(2):
                    here = block(n, r, a, b)
                    below = column_ref[s, :] + row_ref[:, b * HALF : (b + 1) * HALF] - shift
                    value = (block(n, r, b, a).T - 2.0 * here) / below
                    total = total + jnp.sum((value * here).reshape(HALF // 8, 8, HALF), axis=0)
                    value_high, value_low = split(value)
                    t = slice((2 * r + b) * HALF, (2 * r + b + 1) * HALF)
                    amplitudes[n, s, t] = value_high
                    amplitudes[n, V + a * HALF : V + (a + 1) * HALF, t] = value_low
            totals.append(total[:, :128] + total[:, 128:])
        return totals

    def gradient(n):
        for p in range(2):
            s = slice(p * HALF, (p + 1) * HALF)
            both = dot(amplitudes[n], high[:, s], 0)
            value = both[:V] + (both[V:] + dot(amplitudes[n, :V, :], low[:, s], 0))
            if not last:
                grad_ref[n, :, s] = value
                continue
            value = value + before_ref[n, :, s]
            for t in range(COLS):
                to = t + place_ref[0] * (COLS // 2)
                to = to - jnp.where(to >= COLS, COLS, 0)
                for e in range(SLAB // 8):
                    for q in range(HALF // 128):
                        line = n * ROWS + (e * 4 + p * 2 + q) * 8
                        grad_ref[to, line : line + 8, :] = value[
                            t * SLAB + e * 8 : t * SLAB + e * 8 + 8, q * 128 : (q + 1) * 128
                        ]

    energies = []
    coulomb(0)
    coulomb(1)
    for n in range(2):
        energies.append(amplitude(n))
        gradient(n)
    if not last:
        for n in range(2):
            for r in range(ROUNDS):
                energy_ref[2 * r + n] = energies[n][r]
        return
    line = lax.broadcasted_iota(jnp.int32, (8, 128), 0)
    table = jnp.zeros((8, 128), jnp.float32)
    for n in range(2):
        for r in range(ROUNDS):
            value = jnp.sum(early_ref[2 * r + n] + energies[n][r], axis=0, keepdims=True)
            table = jnp.where(line == 2 * r + n, value, table)
    for t in range(COLS):
        grad_ref[t, 2 * ROWS :, :] = table


def unit(stage, *args):
    def body(*refs):
        unit_kernel(stage, *refs)

    early = (shape(2, V, NAUX), shape(2 * ROUNDS, 8, 128))
    return call(
        body,
        shape(COLS, 2 * ROWS + 8, 128) if stage else early,
        "unit",
        args,
        scratch=[pltpu.VMEM((ROUNDS * V, NAUX), jnp.bfloat16)] * 2
        + [pltpu.VMEM((2, V, ROUNDS * V), jnp.float32)]
        + [pltpu.VMEM((2, 2 * V, ROUNDS * V), jnp.bfloat16)],
        scalars=2,
        cost=pl.CostEstimate(
            flops=48 * V * V * NAUX, bytes_accessed=16 * V * NAUX, transcendentals=0
        ),
    )


def finish_kernel(slabs_ref, grad_ref, energy_ref):
    step = pl.program_id(0)
    quad, core = step // 2, step % 2
    line = lax.broadcasted_iota(jnp.int32, (8, 128), 0)
    lane = lax.broadcasted_iota(jnp.int32, (8, 128), 1)
    table = jnp.zeros((8, 128), jnp.float32)
    sources = [x * 8 + y * 4 + quad * 2 + core for x in range(2) for y in range(2)]

    def added(rows):
        values = [slabs_ref[s, rows, :] for s in sources]
        return (values[0] + values[1]) + (values[2] + values[3])

    energy = jnp.sum(added(slice(2 * ROWS, 2 * ROWS + 8)), axis=1, keepdims=True)
    for n in range(2):
        for p in range(4):
            for q in range(4):
                at_row = n * ROWS + (4 * p + q) * 8
                grad_ref[n, 8 * p : 8 * p + 8, q * 128 : (q + 1) * 128] = added(
                    slice(at_row, at_row + 8)
                )
        for r in range(ROUNDS):
            value = energy[2 * r + n : 2 * r + n + 1]
            table = jnp.where((line == r) & (lane == 2 * step + n), value, table)
    table = table[:ROUNDS, :OG] * (1.0 / (V * OG * V))

    @pl.when(step == 0)
    def _():
        energy_ref[...] = table

    @pl.when(step > 0)
    def _():
        energy_ref[...] = energy_ref[...] + table


def finish(slabs):
    return pl.pallas_call(
        finish_kernel,
        out_shape=(shape(OG, SLAB, NAUX), shape(ROUNDS, OG)),
        grid=(OG // 2,),
        in_specs=[pl.BlockSpec(memory_space=pltpu.VMEM)],
        out_specs=(
            pl.BlockSpec((2, SLAB, NAUX), lambda p: (p, 0, 0)),
            pl.BlockSpec((ROUNDS, OG), lambda p: (0, 0)),
        ),
        compiler_params=pltpu.CompilerParams(vmem_limit_bytes=VMEM_LIMIT),
        name="finish",
    )(slabs)


def per_device(factors, occ_energy, virt_energy, pairing):
    group = lax.axis_index("occ")
    v = lax.axis_index("virt")
    core = v & 1
    y = (v >> 1) & 3
    x = v >> 3
    slab = lax.dynamic_slice_in_dim(factors.reshape(OG * V, NAUX), v * PIECE, PIECE, 0)
    mixed = lax.all_to_all(
        slab.reshape(GROUPS, PART, NAUX), "occ", split_axis=0, concat_axis=0, tiled=True
    )
    orbital = (y & 1) * 4 + core * 2
    mates = [pairing[r, group] * OG for r in range(ROUNDS)]
    j = x * 4 + y
    place = jnp.stack(
        [core, group * OG + orbital, group * OG + orbital + 1]
        + [mates[0] + j, mates[1] + j, mates[0] + (j ^ 1), mates[1] + (j ^ 3)]
    ).astype(jnp.int32)
    turned = lax.dynamic_slice_in_dim(
        jnp.concatenate([virt_energy, virt_energy]), core * HALF, V, 0
    )
    column, row = turned.reshape(V, 1), turned.reshape(1, V)
    own = call(
        halves_kernel,
        shape(2, 2 * V, NAUX, dtype=jnp.bfloat16),
        "halves",
        [place, lax.dynamic_slice_in_dim(factors, orbital, 2, 0)],
        scalars=1,
    )
    mixed, own, place, column, row = lax.optimization_barrier((mixed, own, place, column, row))
    picked = call(
        pick_kernel, shape(GROUPS, ROUNDS * PART, NAUX), "pick", [pairing, mixed], scalars=1
    )
    both = lax.all_to_all(picked, "occ", split_axis=0, concat_axis=0, tiled=True)
    *pieces, together = call(
        cut_kernel, (shape(PIECE, NAUX),) * ROUNDS + (shape(ROUNDS, PIECE, NAUX),), "cut", [both]
    )
    others = [swap(piece, flip) for piece, flip in zip(pieces, OTHERS)]
    mates, swapped = [], swap(together, CORE)
    for piece in pieces:
        mates += [piece, swapped]
    grads, energy = unit(0, place, occ_energy, own, *mates, column, row)
    *others, grads = lax.optimization_barrier((*others, grads))
    mates = []
    for piece in others:
        mates += [piece, swap(piece, CORE)]
    started = call(
        near_kernel,
        shape(2 * ROUNDS, V, HALF),
        "near",
        [own, *others],
        cost=pl.CostEstimate(
            flops=12 * V * V * NAUX, bytes_accessed=4 * V * NAUX, transcendentals=0
        ),
    )
    sent = unit(1, place, occ_energy, own, *mates, column, row, started, grads, energy)
    slabs = lax.all_to_all(sent, "virt", split_axis=0, concat_axis=0, tiled=True)
    gradient, pair_energy = finish(slabs)
    return (pair_energy, gradient)


def solution(mesh):
    placed = (P("occ", None, None), P(), P(), P())
    return jax.shard_map(
        per_device,
        mesh=mesh,
        in_specs=placed,
        out_specs=(P(None, "occ"), P("occ", "virt", None)),
        check_vma=False,
    )
```
